512 devices in a mesh: dp: 2 (over x_lo), context: 64 (over z, x_hi, core), tensor: 4 (over y).
Axes of the slice: x: 4 (x_hi: 2, x_lo: 2; x = x_hi * 2 + x_lo), y: 4, z: 16, core: 2. Of those that a mesh axis runs over, the one named last changes fastest.
Arguments:
- streams: bfloat16 [32768, 3, 8192], P(('dp', 'context'), None, 'tensor'), parts along dimension 0, may hold values from -6 to 6
- short_filter: float32 [3, 3, 8192], P(None, None, 'tensor'), may hold values from -3 to 3
- decay_rate: float32 [8192, 16], P('tensor'), as said below
- residue: float32 [8192, 16], P('tensor'), may hold values from -0.26 to 0.26
- bias: float32 [8192], P('tensor'), may hold values from -4 to 4
Outputs:
- gated: bfloat16 [32768, 8192], P(('dp', 'context'), 'tensor'), parts along dimension 0
The draws below stay inside these ranges and needn't reach their ends.
There are 2 independent parts, one for each index of `dp`. The reference program is written for one: setup_inputs(seed, part) draws one part's arguments, and reference() takes and returns one part's arrays. A program takes and returns all parts, laid end to end along the dimension named above; an argument that names none is the same for every part. Nothing has to cross between parts.
Inputs may be any that keep to these rules, and one draw needn't show every extreme that they name: `decay_rate`: positive.
All inputs are finite; a program needn't handle non-finite values.
Results may differ from the reference program's by a relative error of at most 0.0058.
Values may be sent and summed in bfloat16 or wider, within the bound.
A program may use at most 128 MiB of HBM per device.

```python
import jax
import jax.numpy as jnp
from jax import lax

D = 8192
MODES = 16
SEQ = 16384


def mode_table(key):
    rate_key, residue_key = jax.random.split(jax.random.fold_in(key, 29))
    lowest = min(0.5 / SEQ, 1.0 / 60.0)
    highest = 1.0 / 30.0
    spread = jax.random.uniform(rate_key, (D, MODES), jnp.float32)
    rate = jnp.exp(jnp.log(lowest) + spread * (jnp.log(highest) - jnp.log(lowest)))
    noise = jnp.clip(jax.random.normal(residue_key, (D, MODES), jnp.float32), -4.0, 4.0)
    weights = noise * jnp.sqrt(1.0 - jnp.exp(-2.0 * rate)) / jnp.sqrt(jnp.float32(MODES))
    return (rate, weights)


def draw_decay_rate(key, part):
    return mode_table(key)[0]


def draw_residue(key, part):
    return mode_table(key)[1]


def levels(stream_key, shape, shards, smallest, top_value):
    def one(axis_at, blocks):
        draws = jax.random.uniform(jax.random.fold_in(jax.random.fold_in(stream_key, 6), axis_at), (blocks,), jnp.float32, smallest / len(shards), top_value / len(shards))
        return jnp.repeat(jnp.exp(draws), shape[axis_at] // blocks).reshape((-1,) + (1,) * (len(shape) - axis_at - 1))

    factor_of = one(*shards[0])
    for cut in shards[1:]:
        factor_of = factor_of * one(*cut)
    return factor_of


def normal_values(own_key, shape, deviation, bound, shards=(), kind=jnp.bfloat16):
    array = deviation * jax.random.normal(own_key, shape, jnp.float32)
    if shards:
        array = array * levels(own_key, shape, shards, -0.22, 0.18)
    return jnp.clip(array, -bound, bound).astype(kind)


def setup_inputs(seed: int = 0, part: int = 0) -> dict:
    seeds = jax.random.split(jax.random.key(seed), 6)
    part_splits = jax.random.split(jax.random.fold_in(seeds[5], part), 6)
    return {
        "streams": normal_values(part_splits[0], (SEQ, 3, D), 1.0, 6.0, ((0, 64), (2, 4))),
        "short_filter": normal_values(seeds[1], (3, 3, D), 0.6, 3.0, ((2, 4),), jnp.float32),
        "decay_rate": draw_decay_rate(jax.random.fold_in(seeds[5], 71), part),
        "residue": draw_residue(jax.random.fold_in(seeds[5], 71), part),
        "bias": normal_values(seeds[4], (D,), 1.0, 4.0, ((0, 4),), jnp.float32),
    }


def featurize(raw, weights):
    padded = jnp.pad(raw, ((2, 0), (0, 0)))
    return weights[0] * raw + weights[1] * padded[1:-1] + weights[2] * padded[:-2]


def reference(streams, short_filter, decay_rate, residue, bias):
    values = streams.astype(jnp.float32)
    query = featurize(values[:, 0], short_filter[0])
    keyf = featurize(values[:, 1], short_filter[1])
    valuef = featurize(values[:, 2], short_filter[2])
    key_value = lax.optimization_barrier((keyf * valuef).astype(jnp.bfloat16))
    widened = key_value.astype(jnp.float32)
    length = widened.shape[0]
    fft_len = 2 * length
    per_map = 64 if D % 64 == 0 else D
    map_count = D // per_map
    positions = jnp.arange(length, dtype=jnp.float32)
    grouped = widened.reshape(length, map_count, per_map).transpose(1, 0, 2)
    rate_rows = decay_rate.reshape(map_count, per_map, MODES)
    residue_rows = residue.reshape(map_count, per_map, MODES)

    def filter_block(member):
        signal, rates, residues = member
        filter_taps = jnp.sum(residues[None] * jnp.exp(-positions[:, None, None] * rates[None]), axis=2)
        spectrum = jnp.fft.rfft(signal, n=fft_len, axis=0)
        response = jnp.fft.rfft(filter_taps, n=fft_len, axis=0)
        return jnp.fft.irfft(spectrum * response, n=fft_len, axis=0)[:length]

    convolved = lax.map(filter_block, (grouped, rate_rows, residue_rows))
    convolved = convolved.transpose(1, 0, 2).reshape(length, D).astype(jnp.float32)
    mixed = lax.optimization_barrier((convolved + bias * widened).astype(jnp.bfloat16))
    return (query * mixed.astype(jnp.float32)).astype(jnp.bfloat16)
```

```python
import functools

import jax
import jax.numpy as jnp
from jax import lax
from jax.experimental import pallas as pl
from jax.experimental.pallas import tpu as pltpu
from jax.sharding import PartitionSpec as P

F32 = jnp.float32
BF16 = jnp.bfloat16
MESH = pl.DeviceIdType.MESH
LANES = 128


def rows8():
    return lax.broadcasted_iota(jnp.int32, (8, LANES), 0)


def lag_tiles(tile, before):
    row = rows8()
    r1 = pltpu.roll(tile, 1, 0)
    r2 = pltpu.roll(tile, 2, 0)
    lag1 = jnp.where(row < 1, before[0], r1)
    lag2 = jnp.where(row < 2, before[1], r2)
    return lag1, lag2, (r1, r2)


def kernel(
    peers, tokens, groups, modes,
    x_hbm, w_hbm, rate_hbm, res_hbm, bias_hbm, out_hbm,
    w_ref, rate_ref, res_ref, bias_ref, xv, xt, kvt, yt, qf, ov, rate_cm, pole_cm, res_cm, ends, enter,
    rim_out, rim_in, send_c, got_c, scan_c, back_c,
    load_sem, out_sem, rim_sem, sem_a, sem_b,
):
    me = lax.axis_index("context")
    chunk = modes * groups // peers
    halves = groups // 8
    wide = 8 * LANES

    barrier = pltpu.get_barrier_semaphore()

    def greet(k, _):
        pl.semaphore_signal(
            barrier, inc=1, device_id={"context": lax.rem(me + k, peers)}, device_id_type=MESH
        )
        return 0

    tail = pltpu.make_async_copy(x_hbm.at[:, pl.ds(tokens - 16, 16), :], xt, load_sem.at[3])
    tail.start()
    loads = []
    for at, stream in enumerate((1, 2, 0)):
        load = pltpu.make_async_copy(x_hbm.at[stream], xv.at[stream], load_sem.at[at])
        load.start()
        loads.append(load)
    small = []
    pairs = ((rate_hbm, rate_ref), (res_hbm, res_ref), (w_hbm, w_ref), (bias_hbm, bias_ref))
    for at, (src, dst) in enumerate(pairs):
        load = pltpu.make_async_copy(src, dst, load_sem.at[4 + at])
        load.start()
        small.append(load)
    lax.fori_loop(1, peers, greet, 0)

    def prepare(g, _):
        lane = pl.ds(pl.multiple_of(g * LANES, LANES), LANES)
        rate = rate_ref[:, lane]
        where = pl.ds(g, modes, stride=groups)
        rate_cm[where, :] = rate
        pole_cm[where, :] = jnp.exp(-rate)
        res_cm[where, :] = res_ref[:, lane]
        return 0

    for load in small:
        load.wait()
    lax.fori_loop(0, groups, prepare, 0)

    tail.wait()
    wide_row = lax.broadcasted_iota(jnp.int32, (8, LANES * groups), 0)
    last = [xt[i, :, :].astype(F32)[8:16] for i in range(3)]
    rim_out[...] = jnp.where(
        wide_row < 2, pltpu.roll(last[0], 2, 0),
        jnp.where(wide_row < 4, pltpu.roll(last[1], 4, 0), pltpu.roll(last[2], 6, 0)),
    )

    def taps(i, lane):
        return [jnp.broadcast_to(w_ref[i, pl.ds(j, 1), lane], (8, LANES)) for j in range(3)]

    def products(h):
        def group(gi, _):
            g = h * 8 + gi
            lane = pl.ds(pl.multiple_of(g * LANES, LANES), LANES)
            wk, wv = taps(1, lane), taps(2, lane)
            zero = jnp.zeros((8, LANES), F32)
            kb, vb = (zero, zero), (zero, zero)
            for block in range(tokens // 16):
                k16 = xv[1, pl.ds(block * 16, 16), lane].astype(F32)
                v16 = xv[2, pl.ds(block * 16, 16), lane].astype(F32)
                for sub in range(2):
                    k, v = k16[sub * 8:sub * 8 + 8], v16[sub * 8:sub * 8 + 8]
                    k1, k2, kb = lag_tiles(k, kb)
                    v1, v2, vb = lag_tiles(v, vb)
                    kf = wk[0] * k + wk[1] * k1 + wk[2] * k2
                    vf = wv[0] * v + wv[1] * v1 + wv[2] * v2
                    kv = (kf * vf).astype(BF16).astype(F32)
                    if block == 0 and sub == 0:
                        kv = jnp.where(rows8() < 2, 0.0, kv)
                    at = (block * 16 + sub * 8) * groups + g
                    kvt[pl.ds(at, 8, stride=groups), :] = kv
            return 0

        lax.fori_loop(0, 8, group, 0)

    def vregs(ref, h):
        return [ref[pl.ds(m * groups + 8 * h, 8), :] for m in range(modes)]

    def token_rows(t, h):
        return pl.ds(pl.multiple_of(t * groups + 8 * h, 8), 8)

    def end_states(h):
        poles = vregs(pole_cm, h)

        def step(i, states):
            for j in range(8):
                x = kvt[token_rows(i * 8 + j, h), :]
                states = [s * p + x for s, p in zip(states, poles)]
            return states

        states = lax.fori_loop(0, tokens // 8, step, [jnp.zeros((8, LANES), F32)] * modes)
        for m in range(modes):
            ends[pl.ds(m * groups + 8 * h, 8), :] = states[m]

    loads[0].wait()
    loads[1].wait()
    products(0)
    end_states(0)

    pl.semaphore_wait(barrier, peers - 1)
    rim = pltpu.make_async_remote_copy(
        src_ref=rim_out, dst_ref=rim_in, send_sem=rim_sem.at[0], recv_sem=rim_sem.at[1],
        device_id={"context": lax.rem(me + 1, peers)}, device_id_type=MESH,
    )
    rim.start()
    for h in range(1, halves):
        products(h)
        end_states(h)
    loads[2].wait()
    rim.wait()

    def first_tile(g, _):
        lane = pl.ds(pl.multiple_of(g * LANES, LANES), LANES)
        edge = jnp.where(me > 0, rim_in[:, lane], 0.0)
        feats = []
        for i in range(3):
            w = taps(i, lane)
            x = xv[i, pl.ds(0, 16), lane].astype(F32)[0:8]
            before = (pltpu.roll(edge, (8 - 2 * i - 1) % 8, 0), pltpu.roll(edge, (8 - 2 * i) % 8, 0))
            x1, x2, _ = lag_tiles(x, before)
            feats.append(w[0] * x + w[1] * x1 + w[2] * x2)
        kvt[pl.ds(g, 8, stride=groups), :] = (feats[1] * feats[2]).astype(BF16).astype(F32)
        qf[pl.ds(0, 8), lane] = feats[0]
        return 0

    lax.fori_loop(0, groups, first_tile, 0)

    for h in range(halves):
        kv0 = kvt[pl.ds(8 * h, 8), :]
        kv1 = kvt[pl.ds(groups + 8 * h, 8), :]
        for m in range(modes):
            rows = pl.ds(m * groups + 8 * h, 8)
            far = jnp.exp(rate_cm[rows, :] * (2.0 - tokens))
            ends[rows, :] = ends[rows, :] + far * (pole_cm[rows, :] * kv0 + kv1)
    for o in range(peers):
        send_c[o, :, :] = ends[pl.ds(o * chunk, chunk), :]

    def ship(src, dst, sems):
        def one(k, _):
            peer = lax.rem(me + k, peers)
            pltpu.make_async_remote_copy(
                src_ref=src.at[peer], dst_ref=dst.at[me], send_sem=sems.at[0], recv_sem=sems.at[1],
                device_id={"context": peer}, device_id_type=MESH,
            ).start()
            return 0

        lax.fori_loop(1, peers, one, 0)

    def landed(ref, sem):
        part = ref.at[pl.ds(0, peers - 1)]
        pltpu.make_async_copy(part, part, sem).wait()

    ship(send_c, got_c, sem_a)
    got_c[pl.ds(me, 1), :, :] = send_c[pl.ds(me, 1), :, :]

    def local_part(h):
        poles, weights = vregs(pole_cm, h), vregs(res_cm, h)
        direct = bias_ref[pl.ds(8 * h, 8), :]

        def step(i, states):
            for j in range(4):
                rows = token_rows(i * 4 + j, h)
                x = kvt[rows, :]
                states = [s * p + x for s, p in zip(states, poles)]
                parts = [r * s for s, r in zip(states, weights)] + [direct * x]
                while len(parts) > 1:
                    parts = [a + b for a, b in zip(parts[::2], parts[1::2])] + (
                        [parts[-1]] if len(parts) % 2 else []
                    )
                yt[rows, :] = parts[0]
            return states

        lax.fori_loop(0, tokens // 4, step, [jnp.zeros((8, LANES), F32)] * modes)

    def query_part():
        def group(g, _):
            lane = pl.ds(pl.multiple_of(g * LANES, LANES), LANES)
            w = taps(0, lane)
            zero = jnp.zeros((8, LANES), F32)
            before = (zero, zero)
            for block in range(tokens // 16):
                x16 = xv[0, pl.ds(block * 16, 16), lane].astype(F32)
                for sub in range(2):
                    x = x16[sub * 8:sub * 8 + 8]
                    x1, x2, before = lag_tiles(x, before)
                    if block or sub:
                        qf[pl.ds(block * 16 + sub * 8, 8), lane] = w[0] * x + w[1] * x1 + w[2] * x2
            return 0

        lax.fori_loop(0, groups, group, 0)

    local_part(0)
    landed(got_c, sem_a.at[1])
    span = jnp.exp(rate_cm[pl.ds(me * chunk, chunk), :] * (-1.0 * tokens))

    def scan(i, state):
        for j in range(4):
            scan_c[pl.ds(i * 4 + j, 1), :, :] = state[None]
            state = state * span + got_c[i * 4 + j]
        return state

    lax.fori_loop(0, peers // 4, scan, jnp.zeros((chunk, LANES), F32))
    ship(scan_c, back_c, sem_b)
    back_c[pl.ds(me, 1), :, :] = scan_c[pl.ds(me, 1), :, :]
    for h in range(1, halves):
        local_part(h)
    query_part()
    landed(back_c, sem_b.at[1])
    for o in range(peers):
        enter[pl.ds(o * chunk, chunk), :] = back_c[o]

    outs = []
    for h in range(halves):
        poles = vregs(pole_cm, h)
        carried = [
            p * r * s for p, r, s in zip(poles, vregs(res_cm, h), vregs(enter, h))
        ]

        def step(i, terms, h=h, poles=poles):
            for j in range(8):
                rows = token_rows(i * 8 + j, h)
                parts = list(terms)
                while len(parts) > 1:
                    parts = [a + b for a, b in zip(parts[::2], parts[1::2])]
                yt[rows, :] = yt[rows, :] + parts[0]
                terms = [u * p for u, p in zip(terms, poles)]
            return terms

        lax.fori_loop(0, tokens // 8, step, carried)

        def gate(gi, _, h=h):
            g = h * 8 + gi
            lane = pl.ds(pl.multiple_of(g * LANES, LANES), LANES)
            for block in range(tokens // 16):
                at = block * 16
                mixed = jnp.concatenate(
                    [yt[pl.ds((at + sub) * groups + g, 8, stride=groups), :] for sub in (0, 8)], axis=0
                )
                mixed = mixed.astype(BF16).astype(F32)
                ov[pl.ds(at, 16), lane] = (qf[pl.ds(at, 16), lane] * mixed).astype(BF16)
            return 0

        lax.fori_loop(0, 8, gate, 0)
        cols = pl.ds(h * wide, wide)
        out = pltpu.make_async_copy(ov.at[:, cols], out_hbm.at[:, cols], out_sem.at[h])
        out.start()
        outs.append(out)
    landed(send_c, sem_a.at[0])
    landed(scan_c, sem_b.at[0])
    for out in outs:
        out.wait()


def body(streams, short_filter, decay_rate, residue, bias):
    tokens, _, channels = streams.shape
    modes = decay_rate.shape[1]
    groups = channels // LANES
    peers = lax.axis_size("context")
    chunk = modes * groups // peers
    args = (
        streams.transpose(1, 0, 2), short_filter, decay_rate.T, residue.T,
        bias.reshape(groups, LANES),
    )
    hbm = pl.BlockSpec(memory_space=pltpu.HBM)
    table = pltpu.VMEM((modes * groups, LANES), F32)
    chunks = pltpu.VMEM((peers, chunk, LANES), F32)
    return pl.pallas_call(
        functools.partial(kernel, peers, tokens, groups, modes),
        out_shape=jax.ShapeDtypeStruct((tokens, channels), BF16),
        in_specs=[hbm] * 5,
        out_specs=pl.BlockSpec(memory_space=pl.ANY),
        scratch_shapes=[
            pltpu.VMEM(short_filter.shape, F32),
            pltpu.VMEM((modes, channels), F32),
            pltpu.VMEM((modes, channels), F32),
            pltpu.VMEM((groups, LANES), F32),
            pltpu.VMEM((3, tokens, channels), BF16),
            pltpu.VMEM((3, 16, channels), BF16),
            pltpu.VMEM((tokens * groups, LANES), F32),
            pltpu.VMEM((tokens * groups, LANES), F32),
            pltpu.VMEM((tokens, channels), F32),
            pltpu.VMEM((tokens, channels), BF16),
            table, table, table, table, table,
            pltpu.VMEM((8, channels), F32),
            pltpu.VMEM((8, channels), F32),
            chunks, chunks, chunks, chunks,
            pltpu.SemaphoreType.DMA((8,)),
            pltpu.SemaphoreType.DMA((groups // 8,)),
            pltpu.SemaphoreType.DMA((2,)),
            pltpu.SemaphoreType.DMA((2,)),
            pltpu.SemaphoreType.DMA((2,)),
        ],
        compiler_params=pltpu.CompilerParams(
            collective_id=0, has_side_effects=True, vmem_limit_bytes=40 * 2**20
        ),
    )(*[pltpu.with_memory_space_constraint(a, pltpu.HBM) for a in args])


def solution(mesh):
    in_specs = (
        P(("dp", "context"), None, "tensor"),
        P(None, None, "tensor"),
        P("tensor", None),
        P("tensor", None),
        P("tensor"),
    )
    out_specs = P(("dp", "context"), "tensor")
    return jax.shard_map(body, mesh=mesh, in_specs=in_specs, out_specs=out_specs, check_vma=False)
```

```python
import functools

import jax
import jax.numpy as jnp
from jax import lax
from jax.experimental import pallas as pl
from jax.experimental.pallas import tpu as pltpu
from jax.sharding import PartitionSpec as P

F32 = jnp.float32
BF16 = jnp.bfloat16
MESH = pl.DeviceIdType.MESH
LANES = 128


def rows8():
    return lax.broadcasted_iota(jnp.int32, (8, LANES), 0)


def lag_tiles(tile, before):
    row = rows8()
    r1 = pltpu.roll(tile, 1, 0)
    r2 = pltpu.roll(tile, 2, 0)
    lag1 = jnp.where(row < 1, before[0], r1)
    lag2 = jnp.where(row < 2, before[1], r2)
    return lag1, lag2, (r1, r2)


def kernel(
    peers, tokens, groups, modes,
    x_hbm, w_hbm, rate_hbm, res_hbm, bias_hbm, out_hbm,
    w_ref, rate_ref, res_ref, bias_ref, xv, xt, kvt, yt, qf, ov, rate_cm, pole_cm, res_cm, ends, enter,
    rim_out, rim_in, got, total, totals, states_out,
    load_sem, out_sem, rim_sem, got_sem, back_sem, total_send, total_recv, ready,
):
    me = lax.axis_index("context")
    team = modes
    teams = peers // team
    block, spot = me // team, lax.rem(me, team)
    mine = pl.ds(pl.multiple_of(spot * groups, groups), groups)
    halves = groups // 8
    wide = 8 * LANES

    def at_context(rank):
        return {"device_id": {"context": rank}, "device_id_type": MESH}

    def mate(step):
        return block * team + lax.rem(spot + step, team)

    barrier = pltpu.get_barrier_semaphore()

    def greet(rank):
        pl.semaphore_signal(barrier, inc=1, **at_context(rank))

    def greet_mate(step, _):
        greet(mate(step))
        return 0

    tail = pltpu.make_async_copy(x_hbm.at[:, pl.ds(tokens - 16, 16), :], xt, load_sem.at[3])
    tail.start()
    loads = []
    for at, stream in enumerate((1, 2, 0)):
        load = pltpu.make_async_copy(x_hbm.at[stream], xv.at[stream], load_sem.at[at])
        load.start()
        loads.append(load)
    small = []
    pairs = ((rate_hbm, rate_ref), (res_hbm, res_ref), (w_hbm, w_ref), (bias_hbm, bias_ref))
    for at, (src, dst) in enumerate(pairs):
        load = pltpu.make_async_copy(src, dst, load_sem.at[4 + at])
        load.start()
        small.append(load)
    lax.fori_loop(1, team, greet_mate, 0)
    for step in range(1, teams):
        @pl.when(block + step < teams)
        def _(step=step):
            greet(me + step * team)

    @pl.when((spot == 0) & (block > 0))
    def _():
        greet(me - 1)

    expected = team - 1 + block + jnp.where((spot == team - 1) & (block < teams - 1), 1, 0)


    def prepare(g, _):
        lane = pl.ds(pl.multiple_of(g * LANES, LANES), LANES)
        rate = rate_ref[:, lane]
        where = pl.ds(g, modes, stride=groups)
        rate_cm[where, :] = rate
        pole_cm[where, :] = jnp.exp(-rate)
        res_cm[where, :] = res_ref[:, lane]
        return 0

    for load in small:
        load.wait()
    lax.fori_loop(0, groups, prepare, 0)

    tail.wait()
    wide_row = lax.broadcasted_iota(jnp.int32, (8, LANES * groups), 0)
    last = [xt[i, :, :].astype(F32)[8:16] for i in range(3)]
    rim_out[...] = jnp.where(
        wide_row < 2, pltpu.roll(last[0], 2, 0),
        jnp.where(wide_row < 4, pltpu.roll(last[1], 4, 0), pltpu.roll(last[2], 6, 0)),
    )

    def taps(i, lane):
        return [jnp.broadcast_to(w_ref[i, pl.ds(j, 1), lane], (8, LANES)) for j in range(3)]

    def products(h):
        def group(gi, _):
            g = h * 8 + gi
            lane = pl.ds(pl.multiple_of(g * LANES, LANES), LANES)
            wk, wv = taps(1, lane), taps(2, lane)
            zero = jnp.zeros((8, LANES), F32)
            kb, vb = (zero, zero), (zero, zero)
            for block in range(tokens // 16):
                k16 = xv[1, pl.ds(block * 16, 16), lane].astype(F32)
                v16 = xv[2, pl.ds(block * 16, 16), lane].astype(F32)
                for sub in range(2):
                    k, v = k16[sub * 8:sub * 8 + 8], v16[sub * 8:sub * 8 + 8]
                    k1, k2, kb = lag_tiles(k, kb)
                    v1, v2, vb = lag_tiles(v, vb)
                    kf = wk[0] * k + wk[1] * k1 + wk[2] * k2
                    vf = wv[0] * v + wv[1] * v1 + wv[2] * v2
                    kv = (kf * vf).astype(BF16).astype(F32)
                    if block == 0 and sub == 0:
                        kv = jnp.where(rows8() < 2, 0.0, kv)
                    at = (block * 16 + sub * 8) * groups + g
                    kvt[pl.ds(at, 8, stride=groups), :] = kv
            return 0

        lax.fori_loop(0, 8, group, 0)

    def vregs(ref, h):
        return [ref[pl.ds(m * groups + 8 * h, 8), :] for m in range(modes)]

    def token_rows(t, h):
        return pl.ds(pl.multiple_of(t * groups + 8 * h, 8), 8)

    def end_states(h):
        poles = vregs(pole_cm, h)

        def step(i, states):
            for j in range(8):
                x = kvt[token_rows(i * 8 + j, h), :]
                states = [s * p + x for s, p in zip(states, poles)]
            return states

        states = lax.fori_loop(0, tokens // 8, step, [jnp.zeros((8, LANES), F32)] * modes)
        for m in range(modes):
            ends[pl.ds(m * groups + 8 * h, 8), :] = states[m]

    loads[0].wait()
    loads[1].wait()
    products(0)
    end_states(0)

    pl.semaphore_wait(barrier, expected)
    rim = pltpu.make_async_remote_copy(
        src_ref=rim_out, dst_ref=rim_in, send_sem=rim_sem.at[0], recv_sem=rim_sem.at[1],
        **at_context(lax.rem(me + 1, peers)),
    )

    @pl.when(me < peers - 1)
    def _():
        rim.start()

    for step in range(1, teams):
        @pl.when(block >= step)
        def _(step=step):
            pl.semaphore_signal(ready.at[step - 1], inc=1, **at_context(me - step * team))

    for h in range(1, halves):
        products(h)
        end_states(h)
    loads[2].wait()

    @pl.when(me == 0)
    def _():
        rim_in[...] = jnp.zeros_like(rim_in)

    @pl.when(me > 0)
    def _():
        rim.wait_recv()

    def first_tile(g, _):
        lane = pl.ds(pl.multiple_of(g * LANES, LANES), LANES)
        edge = rim_in[:, lane]
        feats = []
        for i in range(3):
            w = taps(i, lane)
            x = xv[i, pl.ds(0, 16), lane].astype(F32)[0:8]
            before = (pltpu.roll(edge, (8 - 2 * i - 1) % 8, 0), pltpu.roll(edge, (8 - 2 * i) % 8, 0))
            x1, x2, _ = lag_tiles(x, before)
            feats.append(w[0] * x + w[1] * x1 + w[2] * x2)
        kvt[pl.ds(g, 8, stride=groups), :] = (feats[1] * feats[2]).astype(BF16).astype(F32)
        qf[pl.ds(0, 8), lane] = feats[0]
        return 0

    lax.fori_loop(0, groups, first_tile, 0)

    for h in range(halves):
        kv0 = kvt[pl.ds(8 * h, 8), :]
        kv1 = kvt[pl.ds(groups + 8 * h, 8), :]
        for m in range(modes):
            rows = pl.ds(m * groups + 8 * h, 8)
            far = jnp.exp(rate_cm[rows, :] * (2.0 - tokens))
            ends[rows, :] = ends[rows, :] + far * (pole_cm[rows, :] * kv0 + kv1)
    def rows_of(to):
        return pl.ds(pl.multiple_of(to * groups, groups), groups)

    def collect(step, _):
        pltpu.make_async_remote_copy(
            src_ref=ends.at[rows_of(lax.rem(spot + step, team))], dst_ref=got.at[spot],
            send_sem=got_sem.at[0], recv_sem=got_sem.at[1], **at_context(mate(step)),
        ).start()
        return 0

    lax.fori_loop(1, team, collect, 0)
    got[pl.ds(spot, 1), :, :] = ends[mine, :][None]

    def team_bytes(sem):
        part = got.at[pl.ds(0, team - 1)]
        return pltpu.make_async_copy(part, part, sem)

    def forward(step):
        return pltpu.make_async_remote_copy(
            src_ref=total, dst_ref=totals.at[step - 1], send_sem=total_send.at[step - 1],
            recv_sem=total_recv.at[step - 1], **at_context(lax.rem(me + step * team, peers)),
        )

    def push(step):
        @pl.when(block + step < teams)
        def _():
            pl.semaphore_wait(ready.at[step - 1], 1)
            forward(step).start()

    blank = [jnp.zeros((8, LANES), F32)] * modes

    def local_part(h, first, last, states):
        poles, weights = vregs(pole_cm, h), vregs(res_cm, h)
        direct = bias_ref[pl.ds(8 * h, 8), :]

        def step(i, states):
            for j in range(4):
                rows = token_rows(i * 4 + j, h)
                x = kvt[rows, :]
                states = [s * p + x for s, p in zip(states, poles)]
                parts = [r * s for s, r in zip(states, weights)] + [direct * x]
                while len(parts) > 1:
                    parts = [a + b for a, b in zip(parts[::2], parts[1::2])] + (
                        [parts[-1]] if len(parts) % 2 else []
                    )
                yt[rows, :] = parts[0]
            return states

        return lax.fori_loop(first // 4, last // 4, step, states)

    def query_part():
        def group(g, _):
            lane = pl.ds(pl.multiple_of(g * LANES, LANES), LANES)
            w = taps(0, lane)
            zero = jnp.zeros((8, LANES), F32)
            before = (zero, zero)
            for block in range(tokens // 16):
                x16 = xv[0, pl.ds(block * 16, 16), lane].astype(F32)
                for sub in range(2):
                    x = x16[sub * 8:sub * 8 + 8]
                    x1, x2, before = lag_tiles(x, before)
                    if block or sub:
                        qf[pl.ds(block * 16 + sub * 8, 8), lane] = w[0] * x + w[1] * x1 + w[2] * x2
            return 0

        lax.fori_loop(0, groups, group, 0)

    half = tokens // 2
    kept = local_part(0, 0, half, blank)
    kept = local_part(0, half, tokens, kept)
    team_bytes(got_sem.at[1]).wait()
    rate = rate_cm[mine, :]
    span = jnp.exp(rate * (-1.0 * tokens))
    leap = jnp.exp(rate * (-1.0 * tokens * team))
    sums = got[0]
    for j in range(1, team):
        sums = sums * span + got[j]
    total[...] = sums
    push(1)
    states_out[0, :, :] = jnp.zeros((groups, LANES), F32)
    for step in range(teams - 1, 0, -1):
        @pl.when(block >= step)
        def _(step=step):
            forward(step).wait_recv()
            states_out[0, :, :] = states_out[0] * leap + totals[step - 1]

    state = states_out[0]
    for j in range(1, team):
        state = state * span + got[j - 1]
        states_out[j, :, :] = state

    def give_back(step, _):
        pltpu.make_async_remote_copy(
            src_ref=states_out.at[lax.rem(spot + step, team)], dst_ref=enter.at[mine],
            send_sem=back_sem.at[0], recv_sem=back_sem.at[1], **at_context(mate(step)),
        ).start()
        return 0

    lax.fori_loop(1, team, give_back, 0)
    enter[mine, :] = states_out[spot]
    for step in range(2, teams):
        push(step)
    for h in range(1, halves):
        kept = local_part(h, 0, half, blank)
        kept = local_part(h, half, tokens, kept)
    query_part()
    team_bytes(back_sem.at[1]).wait()

    outs = []
    for h in range(halves):
        poles = vregs(pole_cm, h)
        carried = [
            p * r * s for p, r, s in zip(poles, vregs(res_cm, h), vregs(enter, h))
        ]

        def step(i, terms, h=h, poles=poles):
            for j in range(8):
                rows = token_rows(i * 8 + j, h)
                parts = list(terms)
                while len(parts) > 1:
                    parts = [a + b for a, b in zip(parts[::2], parts[1::2])]
                yt[rows, :] = yt[rows, :] + parts[0]
                terms = [u * p for u, p in zip(terms, poles)]
            return terms

        lax.fori_loop(0, tokens // 8, step, carried)

        def gate(gi, _, h=h):
            g = h * 8 + gi
            lane = pl.ds(pl.multiple_of(g * LANES, LANES), LANES)
            for block in range(tokens // 16):
                at = block * 16
                mixed = jnp.concatenate(
                    [yt[pl.ds((at + sub) * groups + g, 8, stride=groups), :] for sub in (0, 8)], axis=0
                )
                mixed = mixed.astype(BF16).astype(F32)
                ov[pl.ds(at, 16), lane] = (qf[pl.ds(at, 16), lane] * mixed).astype(BF16)
            return 0

        lax.fori_loop(0, 8, gate, 0)
        cols = pl.ds(h * wide, wide)
        out = pltpu.make_async_copy(ov.at[:, cols], out_hbm.at[:, cols], out_sem.at[h])
        out.start()
        outs.append(out)
    @pl.when(me < peers - 1)
    def _():
        rim.wait_send()

    team_bytes(got_sem.at[0]).wait()
    team_bytes(back_sem.at[0]).wait()
    for step in range(1, teams):
        @pl.when(block + step < teams)
        def _(step=step):
            forward(step).wait_send()

    for out in outs:
        out.wait()


def body(streams, short_filter, decay_rate, residue, bias):
    tokens, _, channels = streams.shape
    modes = decay_rate.shape[1]
    groups = channels // LANES
    peers = lax.axis_size("context")
    teams = peers // modes
    args = (
        streams.transpose(1, 0, 2), short_filter, decay_rate.T, residue.T,
        bias.reshape(groups, LANES),
    )
    hbm = pl.BlockSpec(memory_space=pltpu.HBM)
    table = pltpu.VMEM((modes * groups, LANES), F32)
    pieces = pltpu.VMEM((modes, groups, LANES), F32)
    return pl.pallas_call(
        functools.partial(kernel, peers, tokens, groups, modes),
        out_shape=jax.ShapeDtypeStruct((tokens, channels), BF16),
        in_specs=[hbm] * 5,
        out_specs=pl.BlockSpec(memory_space=pl.ANY),
        scratch_shapes=[
            pltpu.VMEM(short_filter.shape, F32),
            pltpu.VMEM((modes, channels), F32),
            pltpu.VMEM((modes, channels), F32),
            pltpu.VMEM((groups, LANES), F32),
            pltpu.VMEM((3, tokens, channels), BF16),
            pltpu.VMEM((3, 16, channels), BF16),
            pltpu.VMEM((tokens * groups, LANES), F32),
            pltpu.VMEM((tokens * groups, LANES), F32),
            pltpu.VMEM((tokens, channels), F32),
            pltpu.VMEM((tokens, channels), BF16),
            table, table, table, table, table,
            pltpu.VMEM((8, channels), F32),
            pltpu.VMEM((8, channels), F32),
            pieces,
            pltpu.VMEM((groups, LANES), F32),
            pltpu.VMEM((teams - 1, groups, LANES), F32),
            pieces,
            pltpu.SemaphoreType.DMA((8,)),
            pltpu.SemaphoreType.DMA((groups // 8,)),
            pltpu.SemaphoreType.DMA((2,)),
            pltpu.SemaphoreType.DMA((2,)),
            pltpu.SemaphoreType.DMA((2,)),
            pltpu.SemaphoreType.DMA((teams - 1,)),
            pltpu.SemaphoreType.DMA((teams - 1,)),
            pltpu.SemaphoreType.REGULAR((teams - 1,)),
        ],
        compiler_params=pltpu.CompilerParams(
            collective_id=0, has_side_effects=True, vmem_limit_bytes=40 * 2**20
        ),
    )(*[pltpu.with_memory_space_constraint(a, pltpu.HBM) for a in args])


def solution(mesh):
    in_specs = (
        P(("dp", "context"), None, "tensor"),
        P(None, None, "tensor"),
        P("tensor", None),
        P("tensor", None),
        P("tensor"),
    )
    out_specs = P(("dp", "context"), "tensor")
    return jax.shard_map(body, mesh=mesh, in_specs=in_specs, out_specs=out_specs, check_vma=False)
```

```python
import functools

import jax
import jax.numpy as jnp
from jax import lax
from jax.experimental import pallas as pl
from jax.experimental.pallas import tpu as pltpu
from jax.sharding import PartitionSpec as P

F32 = jnp.float32
BF16 = jnp.bfloat16
MESH = pl.DeviceIdType.MESH
LANES = 128


def rows8():
    return lax.broadcasted_iota(jnp.int32, (8, LANES), 0)


def lag_tiles(tile, before):
    row = rows8()
    r1 = pltpu.roll(tile, 1, 0)
    r2 = pltpu.roll(tile, 2, 0)
    lag1 = jnp.where(row < 1, before[0], r1)
    lag2 = jnp.where(row < 2, before[1], r2)
    return lag1, lag2, (r1, r2)


def kernel(
    peers, tokens, groups, modes,
    x_hbm, w_hbm, rate_hbm, res_hbm, bias_hbm, ov,
    w_ref, rate_ref, res_ref, bias_ref, xv, xt, kvt, yt, qf, rate_cm, pole_cm, res_cm, far_cm, ends, enter,
    rim_out, rim_in, got, total, totals, states_out,
    load_sem, rim_sem, got_sem, back_sem, total_send, total_recv, ready,
):
    me = lax.axis_index("context")
    team = modes
    teams = peers // team
    block, spot = me // team, lax.rem(me, team)
    mine = pl.ds(pl.multiple_of(spot * groups, groups), groups)
    halves = groups // 8

    def at_context(rank):
        return {"device_id": {"context": rank}, "device_id_type": MESH}

    def mate(step):
        return block * team + lax.rem(spot + step, team)

    barrier = pltpu.get_barrier_semaphore()

    def greet(rank):
        pl.semaphore_signal(barrier, inc=1, **at_context(rank))

    def greet_mate(k, _):
        greet(mate(k))
        return 0

    tail = pltpu.make_async_copy(x_hbm.at[:, pl.ds(tokens - 16, 16), :], xt, load_sem.at[3])
    tail.start()
    loads = []
    for at, stream in enumerate((1, 2, 0)):
        load = pltpu.make_async_copy(x_hbm.at[stream], xv.at[stream], load_sem.at[at])
        load.start()
        loads.append(load)
    small = []
    pairs = ((rate_hbm, rate_ref), (res_hbm, res_ref), (w_hbm, w_ref), (bias_hbm, bias_ref))
    for at, (src, dst) in enumerate(pairs):
        load = pltpu.make_async_copy(src, dst, load_sem.at[4 + at])
        load.start()
        small.append(load)
    lax.fori_loop(1, team, greet_mate, 0)
    for step in range(1, teams):
        @pl.when(block + step < teams)
        def _(step=step):
            greet(me + step * team)

    @pl.when((spot == 0) & (block > 0))
    def _():
        greet(me - 1)

    expected = team - 1 + block + jnp.where((spot == team - 1) & (block < teams - 1), 1, 0)


    def prepare(g, _):
        lane = pl.ds(pl.multiple_of(g * LANES, LANES), LANES)
        rate = rate_ref[:, lane]
        where = pl.ds(g, modes, stride=groups)
        rate_cm[where, :] = rate
        pole_cm[where, :] = jnp.exp(-rate)
        res_cm[where, :] = res_ref[:, lane]
        far_cm[where, :] = jnp.exp(rate * (2.0 - tokens))
        return 0

    for load in small:
        load.wait()
    lax.fori_loop(0, groups, prepare, 0)

    tail.wait()
    wide_row = lax.broadcasted_iota(jnp.int32, (8, LANES * groups), 0)
    last = [xt[i, :, :].astype(F32)[8:16] for i in range(3)]
    rim_out[...] = jnp.where(
        wide_row < 2, pltpu.roll(last[0], 2, 0),
        jnp.where(wide_row < 4, pltpu.roll(last[1], 4, 0), pltpu.roll(last[2], 6, 0)),
    )

    def taps(i, lane):
        return [jnp.broadcast_to(w_ref[i, pl.ds(j, 1), lane], (8, LANES)) for j in range(3)]

    def products(h):
        def group(gi, _):
            g = h * 8 + gi
            lane = pl.ds(pl.multiple_of(g * LANES, LANES), LANES)
            wk, wv = taps(1, lane), taps(2, lane)
            zero = jnp.zeros((8, LANES), F32)
            kb, vb = (zero, zero), (zero, zero)
            for block in range(tokens // 16):
                k16 = xv[1, pl.ds(block * 16, 16), lane].astype(F32)
                v16 = xv[2, pl.ds(block * 16, 16), lane].astype(F32)
                for sub in range(2):
                    k, v = k16[sub * 8:sub * 8 + 8], v16[sub * 8:sub * 8 + 8]
                    k1, k2, kb = lag_tiles(k, kb)
                    v1, v2, vb = lag_tiles(v, vb)
                    kf = wk[0] * k + wk[1] * k1 + wk[2] * k2
                    vf = wv[0] * v + wv[1] * v1 + wv[2] * v2
                    kv = (kf * vf).astype(BF16).astype(F32)
                    if block == 0 and sub == 0:
                        kv = jnp.where(rows8() < 2, 0.0, kv)
                    at = (block * 16 + sub * 8) * groups + g
                    kvt[pl.ds(at, 8, stride=groups), :] = kv
            return 0

        lax.fori_loop(0, 8, group, 0)

    def vregs(ref, h):
        return [ref[pl.ds(m * groups + 8 * h, 8), :] for m in range(modes)]

    def token_rows(t, h):
        return pl.ds(pl.multiple_of(t * groups + 8 * h, 8), 8)

    def end_states(h):
        poles = vregs(pole_cm, h)

        def step(i, states):
            for j in range(8):
                x = kvt[token_rows(i * 8 + j, h), :]
                states = [s * p + x for s, p in zip(states, poles)]
            return states

        states = lax.fori_loop(0, tokens // 8, step, [jnp.zeros((8, LANES), F32)] * modes)
        for m in range(modes):
            ends[pl.ds(m * groups + 8 * h, 8), :] = states[m]

    loads[0].wait()
    loads[1].wait()
    products(0)
    end_states(0)

    pl.semaphore_wait(barrier, expected)
    rim = pltpu.make_async_remote_copy(
        src_ref=rim_out, dst_ref=rim_in, send_sem=rim_sem.at[0], recv_sem=rim_sem.at[1],
        **at_context(lax.rem(me + 1, peers)),
    )

    @pl.when(me < peers - 1)
    def _():
        rim.start()

    for step in range(1, teams):
        @pl.when(block >= step)
        def _(step=step):
            pl.semaphore_signal(ready.at[step - 1], inc=1, **at_context(me - step * team))

    for h in range(1, halves):
        products(h)
        end_states(h)
    loads[2].wait()

    @pl.when(me == 0)
    def _():
        rim_in[...] = jnp.zeros_like(rim_in)

    @pl.when(me > 0)
    def _():
        rim.wait_recv()

    def first_tile(g, _):
        lane = pl.ds(pl.multiple_of(g * LANES, LANES), LANES)
        edge = rim_in[:, lane]
        feats = []
        for i in (1, 2):
            w = taps(i, lane)
            x = xv[i, pl.ds(0, 16), lane].astype(F32)[0:8]
            before = (pltpu.roll(edge, (8 - 2 * i - 1) % 8, 0), pltpu.roll(edge, (8 - 2 * i) % 8, 0))
            x1, x2, _ = lag_tiles(x, before)
            feats.append(w[0] * x + w[1] * x1 + w[2] * x2)
        kvt[pl.ds(g, 8, stride=groups), :] = (feats[0] * feats[1]).astype(BF16).astype(F32)
        return 0

    lax.fori_loop(0, groups, first_tile, 0)

    for h in range(halves):
        kv0 = kvt[pl.ds(8 * h, 8), :]
        kv1 = kvt[pl.ds(groups + 8 * h, 8), :]
        for m in range(modes):
            rows = pl.ds(m * groups + 8 * h, 8)
            ends[rows, :] = ends[rows, :] + far_cm[rows, :] * (pole_cm[rows, :] * kv0 + kv1)
    def rows_of(to):
        return pl.ds(pl.multiple_of(to * groups, groups), groups)

    def collect(k, _):
        step = k
        pltpu.make_async_remote_copy(
            src_ref=ends.at[rows_of(lax.rem(spot + step, team))], dst_ref=got.at[spot],
            send_sem=got_sem.at[0], recv_sem=got_sem.at[1], **at_context(mate(step)),
        ).start()
        return 0

    lax.fori_loop(1, team, collect, 0)
    got[pl.ds(spot, 1), :, :] = ends[mine, :][None]

    def team_bytes(sem, rows=groups):
        part = got.at[pl.ds(0, team - 1), pl.ds(0, rows)]
        return pltpu.make_async_copy(part, part, sem)

    def forward(step):
        return pltpu.make_async_remote_copy(
            src_ref=total, dst_ref=totals.at[step - 1], send_sem=total_send.at[step - 1],
            recv_sem=total_recv.at[step - 1], **at_context(lax.rem(me + step * team, peers)),
        )

    def push(step):
        @pl.when(block + step < teams)
        def _():
            pl.semaphore_wait(ready.at[step - 1], 1)
            forward(step).start()

    blank = [jnp.zeros((8, LANES), F32)] * modes

    def local_part(h, first, last, states):
        poles, weights = vregs(pole_cm, h), vregs(res_cm, h)
        direct = bias_ref[pl.ds(8 * h, 8), :]

        def step(i, states):
            for j in range(4):
                rows = token_rows(i * 4 + j, h)
                x = kvt[rows, :]
                states = [s * p + x for s, p in zip(states, poles)]
                parts = [r * s for s, r in zip(states, weights)] + [direct * x]
                while len(parts) > 1:
                    parts = [a + b for a, b in zip(parts[::2], parts[1::2])] + (
                        [parts[-1]] if len(parts) % 2 else []
                    )
                yt[rows, :] = parts[0]
            return states

        return lax.fori_loop(first // 4, last // 4, step, states)

    def query_part():
        def group(g, _):
            lane = pl.ds(pl.multiple_of(g * LANES, LANES), LANES)
            w = taps(0, lane)
            edge = rim_in[:, lane]
            before = (pltpu.roll(edge, 7, 0), edge)
            for block in range(tokens // 16):
                x16 = xv[0, pl.ds(block * 16, 16), lane].astype(F32)
                for sub in range(2):
                    x = x16[sub * 8:sub * 8 + 8]
                    x1, x2, before = lag_tiles(x, before)
                    qf[pl.ds(block * 16 + sub * 8, 8), lane] = w[0] * x + w[1] * x1 + w[2] * x2
            return 0

        lax.fori_loop(0, groups, group, 0)

    half = tokens // 2
    kept = local_part(0, 0, half, blank)
    kept = local_part(0, half, tokens, kept)
    team_bytes(got_sem.at[1]).wait()
    rate = rate_cm[mine, :]
    span = jnp.exp(rate * (-1.0 * tokens))
    leap = jnp.exp(rate * (-1.0 * tokens * team))
    sums = got[0]
    for j in range(1, team):
        sums = sums * span + got[j]
    total[...] = sums
    push(1)
    states_out[0, :, :] = jnp.zeros((groups, LANES), F32)
    for step in range(teams - 1, 0, -1):
        @pl.when(block >= step)
        def _(step=step):
            forward(step).wait_recv()
            states_out[0, :, :] = states_out[0] * leap + totals[step - 1]

    state = states_out[0]
    for j in range(1, team):
        state = state * span + got[j - 1]
        states_out[j, :, :] = state

    for h in range(halves):
        def give_back(k, _, h=h):
            step = k
            cols = pl.ds(8 * h, 8)
            rows = pl.ds(pl.multiple_of(spot * groups + 8 * h, 8), 8)
            pltpu.make_async_remote_copy(
                src_ref=states_out.at[lax.rem(spot + step, team), cols], dst_ref=enter.at[rows],
                send_sem=back_sem.at[0, h], recv_sem=back_sem.at[1, h], **at_context(mate(step)),
            ).start()
            return 0

        lax.fori_loop(1, team, give_back, 0)
    enter[mine, :] = states_out[spot]
    for step in range(2, teams):
        push(step)
    for h in range(1, halves):
        kept = local_part(h, 0, half, blank)
        kept = local_part(h, half, tokens, kept)
    query_part()
    def gate(g, first, count):
        lane = pl.ds(pl.multiple_of(g * LANES, LANES), LANES)
        for k in range(count):
            at = pl.multiple_of((first + k) * 16, 16)
            mixed = jnp.concatenate(
                [yt[pl.ds((at + sub) * groups + g, 8, stride=groups), :] for sub in (0, 8)], axis=0
            )
            mixed = mixed.astype(BF16).astype(F32)
            ov[pl.ds(at, 16), lane] = (qf[pl.ds(at, 16), lane] * mixed).astype(BF16)

    steps = tokens // 8
    per_step = 8 * (tokens // 16) // steps
    for h in range(halves):
        team_bytes(back_sem.at[1, h], 8).wait()
        poles = vregs(pole_cm, h)
        carried = [
            p * r * s for p, r, s in zip(poles, vregs(res_cm, h), vregs(enter, h))
        ]

        def step(i, terms, h=h, poles=poles):
            if h:
                blocks = tokens // 16
                place = i * per_step
                gate((h - 1) * 8 + place // blocks, lax.rem(place, blocks), per_step)
            for j in range(8):
                rows = token_rows(i * 8 + j, h)
                parts = list(terms)
                while len(parts) > 1:
                    parts = [a + b for a, b in zip(parts[::2], parts[1::2])]
                yt[rows, :] = yt[rows, :] + parts[0]
                terms = [u * p for u, p in zip(terms, poles)]
            return terms

        lax.fori_loop(0, steps, step, carried)

    def last_gate(gi, _):
        gate((halves - 1) * 8 + gi, 0, tokens // 16)
        return 0

    lax.fori_loop(0, 8, last_gate, 0)

    @pl.when(me < peers - 1)
    def _():
        rim.wait_send()

    team_bytes(got_sem.at[0]).wait()
    for h in range(halves):
        team_bytes(back_sem.at[0, h], 8).wait()
    for step in range(1, teams):
        @pl.when(block + step < teams)
        def _(step=step):
            forward(step).wait_send()


def body(streams, short_filter, decay_rate, residue, bias):
    tokens, _, channels = streams.shape
    modes = decay_rate.shape[1]
    groups = channels // LANES
    peers = lax.axis_size("context")
    teams = peers // modes
    args = (
        streams.transpose(1, 0, 2), short_filter, decay_rate.T, residue.T,
        bias.reshape(groups, LANES),
    )
    hbm = pl.BlockSpec(memory_space=pltpu.HBM)
    table = pltpu.VMEM((modes * groups, LANES), F32)
    pieces = pltpu.VMEM((modes, groups, LANES), F32)
    return pl.pallas_call(
        functools.partial(kernel, peers, tokens, groups, modes),
        out_shape=jax.ShapeDtypeStruct((tokens, channels), BF16),
        in_specs=[hbm] * 5,
        out_specs=pl.BlockSpec(memory_space=pltpu.VMEM),
        scratch_shapes=[
            pltpu.VMEM(short_filter.shape, F32),
            pltpu.VMEM((modes, channels), F32),
            pltpu.VMEM((modes, channels), F32),
            pltpu.VMEM((groups, LANES), F32),
            pltpu.VMEM((3, tokens, channels), BF16),
            pltpu.VMEM((3, 16, channels), BF16),
            pltpu.VMEM((tokens * groups, LANES), F32),
            pltpu.VMEM((tokens * groups, LANES), F32),
            pltpu.VMEM((tokens, channels), F32),
            table, table, table, table, table, table,
            pltpu.VMEM((8, channels), F32),
            pltpu.VMEM((8, channels), F32),
            pieces,
            pltpu.VMEM((groups, LANES), F32),
            pltpu.VMEM((teams - 1, groups, LANES), F32),
            pieces,
            pltpu.SemaphoreType.DMA((8,)),
            pltpu.SemaphoreType.DMA((2,)),
            pltpu.SemaphoreType.DMA((2,)),
            pltpu.SemaphoreType.DMA((2, groups // 8)),
            pltpu.SemaphoreType.DMA((teams - 1,)),
            pltpu.SemaphoreType.DMA((teams - 1,)),
            pltpu.SemaphoreType.REGULAR((teams - 1,)),
        ],
        compiler_params=pltpu.CompilerParams(
            collective_id=0, has_side_effects=True, vmem_limit_bytes=40 * 2**20
        ),
    )(*[pltpu.with_memory_space_constraint(a, pltpu.HBM) for a in args])


def solution(mesh):
    in_specs = (
        P(("dp", "context"), None, "tensor"),
        P(None, None, "tensor"),
        P("tensor", None),
        P("tensor", None),
        P("tensor"),
    )
    out_specs = P(("dp", "context"), "tensor")
    return jax.shard_map(body, mesh=mesh, in_specs=in_specs, out_specs=out_specs, check_vma=False)
```

```python
import functools

import jax
import jax.numpy as jnp
from jax import lax
from jax.experimental import pallas as pl
from jax.experimental.pallas import tpu as pltpu
from jax.sharding import PartitionSpec as P

F32 = jnp.float32
BF16 = jnp.bfloat16
MESH = pl.DeviceIdType.MESH
LANES = 128


def rows8():
    return lax.broadcasted_iota(jnp.int32, (8, LANES), 0)


def lag_tiles(tile, before):
    row = rows8()
    r1 = pltpu.roll(tile, 1, 0)
    r2 = pltpu.roll(tile, 2, 0)
    lag1 = jnp.where(row < 1, before[0], r1)
    lag2 = jnp.where(row < 2, before[1], r2)
    return lag1, lag2, (r1, r2)


def kernel(
    peers, tokens, groups, modes,
    x_hbm, w_hbm, rate_hbm, res_hbm, bias_hbm, ov,
    w_ref, rate_ref, res_ref, bias_ref, xv, xt, kvt, yt, qf, rate_cm, pole_cm, res_cm, far_cm, ends, enter,
    rim_out, rim_in, got, total, totals, states_out,
    load_sem, rim_sem, got_sem, back_sem, total_send, total_recv, ready,
):
    me = lax.axis_index("context")
    team = modes
    teams = peers // team
    block, spot = me // team, lax.rem(me, team)
    mine = pl.ds(pl.multiple_of(spot * groups, groups), groups)
    halves = groups // 8

    def at_context(rank):
        return {"device_id": {"context": rank}, "device_id_type": MESH}

    def mate(step):
        return block * team + lax.rem(spot + step, team)

    barrier = pltpu.get_barrier_semaphore()

    def greet(rank):
        pl.semaphore_signal(barrier, inc=1, **at_context(rank))

    def greet_mate(k, _):
        greet(mate(k))
        return 0

    tail = pltpu.make_async_copy(x_hbm.at[:, pl.ds(tokens - 16, 16), :], xt, load_sem.at[3])
    tail.start()
    loads = []
    for at, stream in enumerate((1, 2, 0)):
        load = pltpu.make_async_copy(x_hbm.at[stream], xv.at[stream], load_sem.at[at])
        load.start()
        loads.append(load)
    small = []
    pairs = ((rate_hbm, rate_ref), (res_hbm, res_ref), (w_hbm, w_ref), (bias_hbm, bias_ref))
    for at, (src, dst) in enumerate(pairs):
        load = pltpu.make_async_copy(src, dst, load_sem.at[4 + at])
        load.start()
        small.append(load)
    lax.fori_loop(1, team, greet_mate, 0)
    for step in range(1, teams):
        @pl.when(block + step < teams)
        def _(step=step):
            greet(me + step * team)

    @pl.when((spot == 0) & (block > 0))
    def _():
        greet(me - 1)

    expected = team - 1 + block + jnp.where((spot == team - 1) & (block < teams - 1), 1, 0)


    def prepare(g, _):
        lane = pl.ds(pl.multiple_of(g * LANES, LANES), LANES)
        rate = rate_ref[:, lane]
        where = pl.ds(g, modes, stride=groups)
        rate_cm[where, :] = rate
        pole_cm[where, :] = jnp.exp(-rate)
        res_cm[where, :] = res_ref[:, lane]
        far_cm[where, :] = jnp.exp(rate * (2.0 - tokens))
        return 0

    for load in small:
        load.wait()
    lax.fori_loop(0, groups, prepare, 0)

    tail.wait()
    wide_row = lax.broadcasted_iota(jnp.int32, (8, LANES * groups), 0)
    last = [xt[i, :, :].astype(F32)[8:16] for i in range(3)]
    rim_out[...] = jnp.where(
        wide_row < 2, pltpu.roll(last[0], 2, 0),
        jnp.where(wide_row < 4, pltpu.roll(last[1], 4, 0), pltpu.roll(last[2], 6, 0)),
    )

    def taps(i, lane):
        return [jnp.broadcast_to(w_ref[i, pl.ds(j, 1), lane], (8, LANES)) for j in range(3)]

    def products(h):
        def group(gi, _):
            g = h * 8 + gi
            lane = pl.ds(pl.multiple_of(g * LANES, LANES), LANES)
            wk, wv = taps(1, lane), taps(2, lane)
            zero = jnp.zeros((8, LANES), F32)
            kb, vb = (zero, zero), (zero, zero)
            for block in range(tokens // 16):
                k16 = xv[1, pl.ds(block * 16, 16), lane].astype(F32)
                v16 = xv[2, pl.ds(block * 16, 16), lane].astype(F32)
                for sub in range(2):
                    k, v = k16[sub * 8:sub * 8 + 8], v16[sub * 8:sub * 8 + 8]
                    k1, k2, kb = lag_tiles(k, kb)
                    v1, v2, vb = lag_tiles(v, vb)
                    kf = wk[0] * k + wk[1] * k1 + wk[2] * k2
                    vf = wv[0] * v + wv[1] * v1 + wv[2] * v2
                    kv = (kf * vf).astype(BF16).astype(F32)
                    if block == 0 and sub == 0:
                        kv = jnp.where(rows8() < 2, 0.0, kv)
                    at = (block * 16 + sub * 8) * groups + g
                    kvt[pl.ds(at, 8, stride=groups), :] = kv
            return 0

        lax.fori_loop(0, 8, group, 0)

    def vregs(ref, h):
        return [ref[pl.ds(m * groups + 8 * h, 8), :] for m in range(modes)]

    def token_rows(t, h):
        return pl.ds(pl.multiple_of(t * groups + 8 * h, 8), 8)

    def end_states(h):
        poles = vregs(pole_cm, h)

        def step(i, states):
            for j in range(8):
                x = kvt[token_rows(i * 8 + j, h), :]
                states = [s * p + x for s, p in zip(states, poles)]
            return states

        states = lax.fori_loop(0, tokens // 8, step, [jnp.zeros((8, LANES), F32)] * modes)
        for m in range(modes):
            ends[pl.ds(m * groups + 8 * h, 8), :] = states[m]

    loads[0].wait()
    loads[1].wait()
    products(0)
    end_states(0)

    pl.semaphore_wait(barrier, expected)
    rim = pltpu.make_async_remote_copy(
        src_ref=rim_out, dst_ref=rim_in, send_sem=rim_sem.at[0], recv_sem=rim_sem.at[1],
        **at_context(lax.rem(me + 1, peers)),
    )

    @pl.when(me < peers - 1)
    def _():
        rim.start()

    for step in range(1, teams):
        @pl.when(block >= step)
        def _(step=step):
            pl.semaphore_signal(ready.at[step - 1], inc=1, **at_context(me - step * team))

    for h in range(1, halves):
        products(h)
        end_states(h)
    loads[2].wait()

    @pl.when(me == 0)
    def _():
        rim_in[...] = jnp.zeros_like(rim_in)

    @pl.when(me > 0)
    def _():
        rim.wait_recv()

    def first_tile(g, _):
        lane = pl.ds(pl.multiple_of(g * LANES, LANES), LANES)
        edge = rim_in[:, lane]
        feats = []
        for i in (1, 2):
            w = taps(i, lane)
            x = xv[i, pl.ds(0, 16), lane].astype(F32)[0:8]
            before = (pltpu.roll(edge, (8 - 2 * i - 1) % 8, 0), pltpu.roll(edge, (8 - 2 * i) % 8, 0))
            x1, x2, _ = lag_tiles(x, before)
            feats.append(w[0] * x + w[1] * x1 + w[2] * x2)
        kvt[pl.ds(g, 8, stride=groups), :] = (feats[0] * feats[1]).astype(BF16).astype(F32)
        return 0

    lax.fori_loop(0, groups, first_tile, 0)

    for h in range(halves):
        kv0 = kvt[pl.ds(8 * h, 8), :]
        kv1 = kvt[pl.ds(groups + 8 * h, 8), :]
        for m in range(modes):
            rows = pl.ds(m * groups + 8 * h, 8)
            ends[rows, :] = ends[rows, :] + far_cm[rows, :] * (pole_cm[rows, :] * kv0 + kv1)
    def rows_of(to):
        return pl.ds(pl.multiple_of(to * groups, groups), groups)

    def collect(k, _):
        step = k
        pltpu.make_async_remote_copy(
            src_ref=ends.at[rows_of(lax.rem(spot + step, team))], dst_ref=got.at[spot],
            send_sem=got_sem.at[0], recv_sem=got_sem.at[1], **at_context(mate(step)),
        ).start()
        return 0

    lax.fori_loop(1, team, collect, 0)
    got[pl.ds(spot, 1), :, :] = ends[mine, :][None]

    def team_bytes(sem, rows=groups):
        part = got.at[pl.ds(0, team - 1), pl.ds(0, rows)]
        return pltpu.make_async_copy(part, part, sem)

    def forward(step):
        return pltpu.make_async_remote_copy(
            src_ref=total, dst_ref=totals.at[step - 1], send_sem=total_send.at[step - 1],
            recv_sem=total_recv.at[step - 1], **at_context(lax.rem(me + step * team, peers)),
        )

    def push(step):
        @pl.when(block + step < teams)
        def _():
            pl.semaphore_wait(ready.at[step - 1], 1)
            forward(step).start()

    blank = [jnp.zeros((8, LANES), F32)] * modes

    def local_part(h, first, last, states):
        poles, weights = vregs(pole_cm, h), vregs(res_cm, h)
        direct = bias_ref[pl.ds(8 * h, 8), :]

        def step(i, states):
            for j in range(4):
                rows = token_rows(i * 4 + j, h)
                x = kvt[rows, :]
                states = [s * p + x for s, p in zip(states, poles)]
                parts = [r * s for s, r in zip(states, weights)] + [direct * x]
                while len(parts) > 1:
                    parts = [a + b for a, b in zip(parts[::2], parts[1::2])] + (
                        [parts[-1]] if len(parts) % 2 else []
                    )
                yt[rows, :] = parts[0]
            return states

        return lax.fori_loop(first // 4, last // 4, step, states)

    def query_part():
        def group(g, _):
            lane = pl.ds(pl.multiple_of(g * LANES, LANES), LANES)
            w = taps(0, lane)
            edge = rim_in[:, lane]
            before = (pltpu.roll(edge, 7, 0), edge)
            for block in range(tokens // 16):
                x16 = xv[0, pl.ds(block * 16, 16), lane].astype(F32)
                for sub in range(2):
                    x = x16[sub * 8:sub * 8 + 8]
                    x1, x2, before = lag_tiles(x, before)
                    qf[pl.ds(block * 16 + sub * 8, 8), lane] = w[0] * x + w[1] * x1 + w[2] * x2
            return 0

        lax.fori_loop(0, groups, group, 0)

    half = tokens // 2
    kept = local_part(0, 0, half, blank)
    kept = local_part(0, half, tokens, kept)
    team_bytes(got_sem.at[1]).wait()
    rate = rate_cm[mine, :]
    span = jnp.exp(rate * (-1.0 * tokens))
    leap = jnp.exp(rate * (-1.0 * tokens * team))
    sums = got[0]
    for j in range(1, team):
        sums = sums * span + got[j]
    total[...] = sums
    push(1)
    states_out[0, :, :] = jnp.zeros((groups, LANES), F32)
    for step in range(teams - 1, 0, -1):
        @pl.when(block >= step)
        def _(step=step):
            forward(step).wait_recv()
            states_out[0, :, :] = states_out[0] * leap + totals[step - 1]

    state = states_out[0]
    for j in range(1, team):
        state = state * span + got[j - 1]
        states_out[j, :, :] = state

    for h in range(halves):
        def give_back(k, _, h=h):
            step = k
            cols = pl.ds(8 * h, 8)
            rows = pl.ds(pl.multiple_of(spot * groups + 8 * h, 8), 8)
            pltpu.make_async_remote_copy(
                src_ref=states_out.at[lax.rem(spot + step, team), cols], dst_ref=enter.at[rows],
                send_sem=back_sem.at[0, h], recv_sem=back_sem.at[1, h], **at_context(mate(step)),
            ).start()
            return 0

        lax.fori_loop(1, team, give_back, 0)
    enter[mine, :] = states_out[spot]
    for step in range(2, teams):
        push(step)
    for h in range(1, halves):
        kept = local_part(h, 0, half, blank)
        kept = local_part(h, half, tokens, kept)
    query_part()
    def gate(g, first, count):
        lane = pl.ds(pl.multiple_of(g * LANES, LANES), LANES)
        for k in range(count):
            at = pl.multiple_of((first + k) * 16, 16)
            mixed = jnp.concatenate(
                [yt[pl.ds((at + sub) * groups + g, 8, stride=groups), :] for sub in (0, 8)], axis=0
            )
            mixed = mixed.astype(BF16).astype(F32)
            ov[pl.ds(at, 16), lane] = (qf[pl.ds(at, 16), lane] * mixed).astype(BF16)

    steps = tokens // 8
    per_step = 8 * (tokens // 16) // steps
    for h in range(halves):
        team_bytes(back_sem.at[1, h], 8).wait()
        poles = vregs(pole_cm, h)
        carried = [
            p * r * s for p, r, s in zip(poles, vregs(res_cm, h), vregs(enter, h))
        ]

        def step(i, terms, h=h, poles=poles):
            if h:
                blocks = tokens // 16
                place = i * per_step
                gate((h - 1) * 8 + place // blocks, lax.rem(place, blocks), per_step)
            if h == halves - 1:
                for q in range(4):
                    gate(h * 8 + lax.rem(i, 2) * 4 + q, jnp.maximum(i // 2 - 1, 0), 1)
            for j in range(8):
                rows = token_rows(i * 8 + j, h)
                parts = list(terms)
                while len(parts) > 1:
                    parts = [a + b for a, b in zip(parts[::2], parts[1::2])]
                yt[rows, :] = yt[rows, :] + parts[0]
                terms = [u * p for u, p in zip(terms, poles)]
            return terms

        lax.fori_loop(0, steps, step, carried)

    def last_gate(gi, _):
        gate((halves - 1) * 8 + gi, tokens // 16 - 1, 1)
        return 0

    lax.fori_loop(0, 8, last_gate, 0)

    @pl.when(me < peers - 1)
    def _():
        rim.wait_send()

    team_bytes(got_sem.at[0]).wait()
    for h in range(halves):
        team_bytes(back_sem.at[0, h], 8).wait()
    for step in range(1, teams):
        @pl.when(block + step < teams)
        def _(step=step):
            forward(step).wait_send()


def body(streams, short_filter, decay_rate, residue, bias):
    tokens, _, channels = streams.shape
    modes = decay_rate.shape[1]
    groups = channels // LANES
    peers = lax.axis_size("context")
    teams = peers // modes
    args = (
        streams.transpose(1, 0, 2), short_filter, decay_rate.T, residue.T,
        bias.reshape(groups, LANES),
    )
    hbm = pl.BlockSpec(memory_space=pltpu.HBM)
    table = pltpu.VMEM((modes * groups, LANES), F32)
    pieces = pltpu.VMEM((modes, groups, LANES), F32)
    return pl.pallas_call(
        functools.partial(kernel, peers, tokens, groups, modes),
        out_shape=jax.ShapeDtypeStruct((tokens, channels), BF16),
        in_specs=[hbm] * 5,
        out_specs=pl.BlockSpec(memory_space=pltpu.VMEM),
        scratch_shapes=[
            pltpu.VMEM(short_filter.shape, F32),
            pltpu.VMEM((modes, channels), F32),
            pltpu.VMEM((modes, channels), F32),
            pltpu.VMEM((groups, LANES), F32),
            pltpu.VMEM((3, tokens, channels), BF16),
            pltpu.VMEM((3, 16, channels), BF16),
            pltpu.VMEM((tokens * groups, LANES), F32),
            pltpu.VMEM((tokens * groups, LANES), F32),
            pltpu.VMEM((tokens, channels), F32),
            table, table, table, table, table, table,
            pltpu.VMEM((8, channels), F32),
            pltpu.VMEM((8, channels), F32),
            pieces,
            pltpu.VMEM((groups, LANES), F32),
            pltpu.VMEM((teams - 1, groups, LANES), F32),
            pieces,
            pltpu.SemaphoreType.DMA((8,)),
            pltpu.SemaphoreType.DMA((2,)),
            pltpu.SemaphoreType.DMA((2,)),
            pltpu.SemaphoreType.DMA((2, groups // 8)),
            pltpu.SemaphoreType.DMA((teams - 1,)),
            pltpu.SemaphoreType.DMA((teams - 1,)),
            pltpu.SemaphoreType.REGULAR((teams - 1,)),
        ],
        compiler_params=pltpu.CompilerParams(
            collective_id=0, has_side_effects=True, vmem_limit_bytes=40 * 2**20
        ),
    )(*[pltpu.with_memory_space_constraint(a, pltpu.HBM) for a in args])


def solution(mesh):
    in_specs = (
        P(("dp", "context"), None, "tensor"),
        P(None, None, "tensor"),
        P("tensor", None),
        P("tensor", None),
        P("tensor"),
    )
    out_specs = P(("dp", "context"), "tensor")
    return jax.shard_map(body, mesh=mesh, in_specs=in_specs, out_specs=out_specs, check_vma=False)
```
